32 devices in a mesh: row: 4 (over z), col: 8 (over y, x, core).
Axes of the slice: x: 2, y: 2, z: 4, core: 2. Of those that a mesh axis runs over, the one named last changes fastest.
Arguments:
- dec_src: float32 [2304, 8192], P('col', 'row'), may hold values from -6 to 6
- enc_tgt: float32 [2304, 16384], P('row', 'col'), may hold values from -0.125 to 0.125
- src_coacts: float32 [512, 8192], P('col', 'row'), may hold values from -6 to 6
- tgt_coacts: float32 [512, 16384], P('row', 'col'), may hold values from -6 to 6
- eval_src: float32 [512, 8192], P('col', 'row'), may hold values from -6 to 6
- enc_bias: float32 [16384], P('col'), may hold values from -0.5 to 0.5
- dec_tgt: float32 [2304, 16384], P('row', 'col'), may hold values from -0.046875 to 0.046875
- tile_mask: int32 [128, 256], P('row', 'col'), may hold values from 0 to 1, as said below
Outputs:
- recon: float32 [512, 2304], P('col', 'row')
The draws below stay inside these ranges and needn't reach their ends.
Inputs may be any that keep to these rules, and one draw needn't show every extreme that they name: `tile_mask`: 1 keeps a tile, 0 prunes it; the share of kept tiles differs between regions of the grid.
All inputs are finite; a program needn't handle non-finite values.
Results may differ from the reference program's by a relative error of at most 0.0003.
Values sent between devices are 32-bit elements; how exact they have to be, the bound alone decides.
A program may use at most 192 MiB of HBM per device.

```python
import jax
import jax.numpy as jnp
from jax import lax

D = 2304
T_SIZE = 16384
S = 8192
TILE = 64
NG = 512
E = 512
N_ROW = 4


def draw_tile_mask(key, part):
    block_rows = jnp.arange(S // TILE, dtype=jnp.int32)[:, None]
    block_cols = jnp.arange(T_SIZE // TILE, dtype=jnp.int32)[None, :]
    level = block_rows * 8 // (S // TILE) + block_cols * 8 // (T_SIZE // TILE)
    percent = 15 + level * 5
    rolled = jax.random.randint(jax.random.fold_in(key, 11), (S // TILE, T_SIZE // TILE), 0, 100, dtype=jnp.int32)
    return (rolled < percent).astype(jnp.int32)


def levels(rng, shape, shards, low, top_value):
    def one(position, shards_of):
        draws = jax.random.uniform(jax.random.fold_in(jax.random.fold_in(rng, 6), position), (shards_of,), jnp.float32, low / len(shards), top_value / len(shards))
        return jnp.repeat(jnp.exp(draws), shape[position] // shards_of).reshape((-1,) + (1,) * (len(shape) - position - 1))

    gain = one(*shards[0])
    for cut in shards[1:]:
        gain = gain * one(*cut)
    return gain


def centred(key, shape, scale, reach, pieces=(), kind=jnp.bfloat16):
    factor_of = levels(key, shape, pieces, -0.22, 0.18) if pieces else 1.0
    drawn = jax.random.normal(key, shape, jnp.float32) * scale * factor_of
    return jnp.minimum(jnp.maximum(drawn, -reach), reach).astype(kind)


def setup_inputs(seed: int = 0) -> dict:
    key_of = jax.random.split(jax.random.key(seed), 9)
    return {
        "dec_src": centred(key_of[0], (D, S), 1.0, 6.0, ((0, 8), (1, 4)), jnp.float32),
        "enc_tgt": centred(key_of[1], (D, T_SIZE), D ** -0.5, 0.125, ((0, 4), (1, 8)), jnp.float32),
        "src_coacts": centred(key_of[2], (NG, S), 1.0, 6.0, ((0, 8), (1, 4)), jnp.float32),
        "tgt_coacts": centred(key_of[3], (NG, T_SIZE), 1.0, 6.0, ((0, 4), (1, 8)), jnp.float32),
        "eval_src": centred(key_of[4], (E, S), 1.0, 6.0, ((0, 8), (1, 4)), jnp.float32),
        "enc_bias": jnp.clip(jax.random.uniform(key_of[5], (T_SIZE,), jnp.float32, -0.5, 0.5) * levels(key_of[5], (T_SIZE,), ((0, 8),), -0.4, 0.0), -0.5, 0.5),
        "dec_tgt": centred(key_of[6], (D, T_SIZE), T_SIZE ** -0.5, 0.046875, ((0, 4), (1, 8)), jnp.float32),
        "tile_mask": draw_tile_mask(jax.random.fold_in(key_of[8], 71), 0),
    }


PRECISE = lax.Precision.HIGHEST

def reference(dec_src, enc_tgt, src_coacts, tgt_coacts, eval_src, enc_bias, dec_tgt, tile_mask):
    block_rows = S // N_ROW
    tile_rows = block_rows // TILE
    tile_cols = T_SIZE // TILE
    norm_gram = 1.0 / jnp.sqrt(jnp.float32(NG))

    def accumulate(pre_acts, block_index):
        offset = (block_index * block_rows).astype(jnp.int32)
        dec_block = lax.dynamic_slice_in_dim(dec_src, offset, block_rows, 1)
        virtual = lax.dot_general(dec_block, enc_tgt, (((0,), (0,)), ((), ())), precision=PRECISE, preferred_element_type=jnp.float32)
        src_block = lax.dynamic_slice_in_dim(src_coacts, offset, block_rows, 1)
        coact = lax.dot_general(src_block, tgt_coacts, (((0,), (0,)), ((), ())), precision=PRECISE, preferred_element_type=jnp.float32) * norm_gram
        mask_block = lax.dynamic_slice_in_dim(tile_mask, (block_index * tile_rows).astype(jnp.int32), tile_rows, 0).astype(jnp.float32)
        weighted = ((virtual * coact).reshape(tile_rows, TILE, tile_cols, TILE) * mask_block[:, None, :, None]).reshape(block_rows, T_SIZE)
        eval_block = lax.dynamic_slice_in_dim(eval_src, offset, block_rows, 1)
        return (pre_acts + jnp.dot(eval_block, weighted, precision=PRECISE, preferred_element_type=jnp.float32), None)
    pre_acts, _ = lax.scan(accumulate, jnp.zeros((E, T_SIZE), jnp.float32), jnp.arange(N_ROW, dtype=jnp.int32))
    hidden = jnp.maximum(pre_acts / jnp.sqrt(jnp.float32(S)) + enc_bias[None, :], 0.0)
    return lax.dot_general(hidden, dec_tgt, (((1,), (1,)), ((), ())), precision=PRECISE, preferred_element_type=jnp.float32)
```

```python
import functools

import jax
import jax.numpy as jnp
from jax import lax
from jax.experimental import pallas as pl
from jax.experimental.pallas import tpu as pltpu
from jax.sharding import PartitionSpec as P


CHUNKS = 2


def split(value):
    high = value.astype(jnp.bfloat16)
    return high, (value - high.astype(jnp.float32)).astype(jnp.bfloat16)


def dot3(left, rows, right, left_dim, right_dim):
    def one(a, b):
        return lax.dot_general(a, b, (((left_dim,), (right_dim,)), ((), ())), preferred_element_type=jnp.float32)

    both = one(left, right[0])
    return both[:rows] + (both[rows:] + one(left[:rows], right[1]))


def prepare(enc_rows, row, *refs):
    blocks, (enc_both, tgt_both, ordered) = refs[:-3], refs[-3:]
    n_row, height = len(blocks), ordered.shape[2]
    for step, block in enumerate(blocks):
        ordered[lax.rem(row[0] + n_row - step, n_row)] = block[...]
    for rows, out in ((slice(None, enc_rows), enc_both), (slice(enc_rows, None), tgt_both)):
        out[:height], out[height:] = split(ordered[:, rows, :].reshape(-1, height).T)


def prepare_target(row, blocks, enc_rows):
    n_row = len(blocks)
    rows, height = blocks[0].shape
    shapes = [(2 * height, n_row * n) for n in (enc_rows, rows - enc_rows)]
    return pl.pallas_call(
        functools.partial(prepare, enc_rows),
        in_specs=[pl.BlockSpec(memory_space=pltpu.SMEM)] + [pl.BlockSpec(memory_space=pltpu.VMEM)] * n_row,
        out_specs=[pl.BlockSpec(memory_space=pltpu.VMEM)] * 2,
        out_shape=[jax.ShapeDtypeStruct(shape, jnp.bfloat16) for shape in shapes],
        scratch_shapes=[pltpu.VMEM((n_row, rows, height), jnp.float32)],
        compiler_params=pltpu.CompilerParams(vmem_limit_bytes=60 * 1024 * 1024),
        cost_estimate=pl.CostEstimate(flops=0, bytes_accessed=8 * n_row * rows * height, transcendentals=0),
    )(row.reshape(1), *blocks)


def weigh(dec_rows, src_rows, norm, source, enc_both, tgt_both, mask, out):
    width = source.shape[2]
    height = out.shape[0]

    @pl.when(pl.program_id(0) == 0)
    def _():
        out[...] = jnp.zeros_like(out)

    dec = split(source[:, :dec_rows, :].reshape(-1, width))
    virtual = dot3(enc_both[...], height, dec, 1, 0)
    src = split(source[:, dec_rows : dec_rows + src_rows, :].reshape(-1, width))
    coact = dot3(tgt_both[...], height, src, 1, 0) * norm
    tiles = mask.shape[1]
    keep = jnp.broadcast_to(mask[0][:, None, :], (tiles, height // tiles, width)).reshape(height, width)
    weighted = jnp.concatenate(split(virtual * coact * keep), axis=0)
    evals = split(source[:, dec_rows + src_rows :, :].reshape(-1, width))
    out[...] += dot3(weighted, height, evals, 1, 1)


def partial_pre(source, target, mask, dec_rows, src_rows, norm):
    n_col, packed, count = source.shape
    height = target[0].shape[0] // 2
    depth, stats = target[0].shape[1], target[1].shape[1]
    width = min(256, count)
    evals = n_col * (packed - dec_rows - src_rows)
    return pl.pallas_call(
        functools.partial(weigh, dec_rows, src_rows, norm),
        grid=(count // width,),
        in_specs=[
            pl.BlockSpec((n_col, packed, width), lambda i: (0, 0, i)),
            pl.BlockSpec(target[0].shape, lambda i: (0, 0)),
            pl.BlockSpec(target[1].shape, lambda i: (0, 0)),
            pl.BlockSpec((1, mask.shape[1], width), lambda i: (0, 0, i)),
        ],
        out_specs=pl.BlockSpec((height, evals), lambda i: (0, 0)),
        out_shape=jax.ShapeDtypeStruct((height, evals), jnp.float32),
        compiler_params=pltpu.CompilerParams(vmem_limit_bytes=60 * 1024 * 1024),
        cost_estimate=pl.CostEstimate(
            flops=6 * count * height * (depth + stats + evals),
            bytes_accessed=4 * (source.size + height * (depth + stats)),
            transcendentals=0,
        ),
    )(source, *target, mask)


def layer(n_row, dec_src, enc_tgt, src_coacts, tgt_coacts, eval_src, enc_bias, dec_tgt, tile_mask):
    members = n_row // 2
    src_count = dec_src.shape[1]
    half = enc_tgt.shape[1] // 2
    chunk = half // CHUNKS
    piece = chunk // members
    dec_rows, src_rows, enc_rows = dec_src.shape[0], src_coacts.shape[0], enc_tgt.shape[0]
    stats = tgt_coacts.shape[0] * n_row
    tile = src_count // tile_mask.shape[0]
    row = lax.axis_index("row")
    parity = lax.rem(row, 2)
    group = row // 2
    norm = 1.0 / float(stats) ** 0.5

    packed = jnp.concatenate([dec_src, src_coacts, eval_src], axis=0)
    packed_other = lax.ppermute(packed, "row", [(r, r ^ 1) for r in range(n_row)])
    mask_t = tile_mask.T.astype(jnp.float32)
    mask_here = lax.dynamic_slice_in_dim(mask_t, parity * (half // tile), half // tile, 0)
    mask_there = lax.dynamic_slice_in_dim(mask_t, (1 - parity) * (half // tile), half // tile, 0)
    mask_other = lax.ppermute(mask_there, "row", [(r, r ^ 1) for r in range(n_row)])

    sources = [(lax.all_gather(packed, "col", axis=0, tiled=False), jnp.repeat(mask_here, tile, axis=1))]
    gathered = lax.all_gather(packed_other, "col", axis=0, tiled=False)
    sources.append((gathered, jnp.repeat(mask_other, tile, axis=1)))

    targets = []
    for k in range(CHUNKS):
        def columns(side):
            start = side * half + k * chunk
            return jnp.concatenate(
                [lax.dynamic_slice_in_dim(a, start, chunk, 1) for a in (enc_tgt, tgt_coacts)], axis=0
            )

        same, across = columns(parity), columns(1 - parity)
        blocks = []
        for step in range(n_row):
            block = same if step % 2 == 0 else across
            if step:
                block = lax.ppermute(block, "row", [(r, (r + step) % n_row) for r in range(n_row)])
            blocks.append(block)
        targets.append(prepare_target(row, blocks, enc_rows))

    scale = 1.0 / jnp.sqrt(jnp.float32(src_count * n_row))
    recon_part = None
    for k in range(CHUNKS):
        partial = None
        for gathered, mask in sources:
            rows = chunk // tile
            term = partial_pre(gathered, targets[k], mask[None, k * rows : (k + 1) * rows], dec_rows, src_rows, norm)
            partial = term if partial is None else partial + term
        total = lax.dynamic_slice_in_dim(partial, group * piece, piece, 0)
        for step in range(1, members):
            target = lax.rem(group + step, members)
            sent = lax.dynamic_slice_in_dim(partial, target * piece, piece, 0)
            arrived = lax.ppermute(sent, "row", [(r, (r + 2 * step) % n_row) for r in range(n_row)])
            total = total + arrived
        bias = lax.dynamic_slice_in_dim(enc_bias, parity * half + k * chunk + group * piece, piece, 0)
        hidden = jnp.maximum(total * scale + bias[:, None], 0.0)
        hidden_all = lax.all_gather(hidden, "row", axis=0, tiled=True)
        starts = [(r % 2) * half + k * chunk + (r // 2) * piece for r in range(n_row)]
        dec_part = jnp.concatenate([dec_tgt[:, s : s + piece] for s in starts], axis=1)
        term = lax.dot_general(
            hidden_all, dec_part, (((0,), (1,)), ((), ())),
            precision=lax.Precision.HIGH, preferred_element_type=jnp.float32,
        )
        recon_part = term if recon_part is None else recon_part + term
    return lax.psum_scatter(recon_part, "col", scatter_dimension=0, tiled=True)


def solution(mesh):
    return jax.shard_map(
        functools.partial(layer, mesh.shape["row"]),
        mesh=mesh,
        in_specs=(
            P("col", "row"),
            P("row", "col"),
            P("col", "row"),
            P("row", "col"),
            P("col", "row"),
            P("col"),
            P("row", "col"),
            P("row", "col"),
        ),
        out_specs=P("col", "row"),
        check_vma=False,
    )
```
